32 devices in a mesh: panel: 8 (over z, y), obs: 4 (over x, core).
Axes of the slice: x: 2, y: 2, z: 4, core: 2. Of those that a mesh axis runs over, the one named last changes fastest.
Arguments:
- flow_blocks: bfloat16 [1024, 4, 1280], P('panel'), may hold values from -6 to 6
- interp_weights: bfloat16 [32, 128, 512], P(('panel', 'obs')), may hold values from -0.25 to 0.25
- donor_owner: int32 [4096, 1], P(('panel', 'obs')), may hold values from 0 to 7; in each aligned block of 128 rows (0 to 127, 128 to 255, ...) at most 24 rows name the same one
- donor_block: int32 [4096], P(('panel', 'obs')), may hold values from 0 to 127
- panel_normals: float32 [3, 4096], P(None, ('panel', 'obs')), may hold values from -3 to 3
- panel_points: float32 [3, 4096], P(None, ('panel', 'obs')), may hold values from -1 to 1
- observer_points: float32 [3, 1024], P(None, 'obs'), may hold values from -12 to 12, as said below
Outputs:
- pressure: float32 [128, 1024], P('panel', 'obs')
The draws below stay inside these ranges and needn't reach their ends.
Inputs may be any that keep to these rules, and one draw needn't show every extreme that they name: `donor_owner`: within the rows of one device, no owner index is named by more than 24 rows; some devices' rows name one owner exactly 24 times. `observer_points`: every observer lies between 6 and 12 from the anchor.
All inputs are finite; a program needn't handle non-finite values.
Results may differ from the reference program's by a relative error of at most 0.0003.
Values may be sent and summed in bfloat16 or wider, within the bound.
A program may use at most 64 MiB of HBM per device.

```python
import math
import jax
import jax.numpy as jnp
import numpy as np
from jax import lax

NV = 5
NT = 256
HARM = 64
TILE = 128
SLOTS = 128
CB = 4
GB_DEV = 128
TILE_DEV = 1
TILES = 32
PANELS = 4096
BLOCKS = 1024
OBS = 1024
CAP = 24
N_PANEL = 8


def draw_observer_points(key, part):
    key_height, key_turn, key_radius = jax.random.split(key, 3)
    height = jax.random.uniform(key_height, (OBS,), jnp.float32, -1.0, 1.0)
    turn = jax.random.uniform(key_turn, (OBS,), jnp.float32, -math.pi, math.pi)
    radius = jax.random.uniform(key_radius, (OBS,), jnp.float32, 6.0, 12.0)
    side = jnp.sqrt(jnp.maximum(1.0 - height * height, 0.0))
    return jnp.stack([radius * side * jnp.cos(turn), radius * side * jnp.sin(turn), radius * height])


def plant(array, key, smallest, top_value):
    shape = array.shape
    spot = [jax.random.randint(jax.random.fold_in(key, axis), (), 0, shape[axis]) for axis in range(len(shape))]
    array = array.at[tuple(spot)].set(smallest)
    longest = shape.index(max(shape))
    spot[longest] = (spot[longest] + 1) % shape[longest]
    return array.at[tuple(spot)].set(top_value)


def level_of(stream_key, dims, cuts, least, high):
    gain = 1.0
    for axis_at, shards_of in cuts:
        heights = jax.random.uniform(jax.random.fold_in(jax.random.fold_in(stream_key, 6), axis_at), (shards_of,), jnp.float32, least / len(cuts), high / len(cuts))
        gain = gain * jnp.repeat(jnp.exp(heights), dims[axis_at] // shards_of).reshape((-1,) + (1,) * (len(dims) - 1 - axis_at))
    return gain


def assign_block(stream_key, own, number, rows, amount, top, limit, slope):
    sequence = jax.random.permutation(stream_key, amount)
    packed, ordinary = shares(amount, rows * top, limit, slope, True), shares(amount, rows * top, limit, slope, False)
    places = jnp.arange(amount)

    def named(tallies, turn):
        used = int((tallies > 0).sum())
        fixed = max(1, used // 4)
        moved = fixed + (places - fixed + turn * (used - fixed)) % max(1, amount - fixed)
        return jnp.zeros((amount,), jnp.int32).at[sequence[jnp.where(places < fixed, places, moved)]].set(jnp.asarray(tallies, jnp.int32))

    tallies = jnp.where(number % 4 == 0, named(packed, number // 4), named(ordinary, number - number // 4 - 1))
    mixed = jax.random.permutation(jax.random.fold_in(own, 3), amount)
    donor, sink = mixed[0:amount // 2 * 2:2], mixed[1:amount // 2 * 2:2]
    slack = jnp.minimum(tallies[donor] - 1, limit - tallies[sink]) // 2
    slack = jnp.where((donor == sequence[0]) | (sink == sequence[0]) | (tallies[sink] == 0), 0, jnp.maximum(slack, 0))
    moved = jax.random.randint(jax.random.fold_in(own, 4), (amount // 2,), 0, 1 << 20) % (slack + 1)
    tallies = tallies.at[donor].add(-moved).at[sink].add(moved)
    items = jnp.searchsorted(jnp.cumsum(tallies), jnp.arange(rows * top), side="right").astype(jnp.int32)
    table = items.reshape(top, rows).T
    table = table[jax.random.permutation(jax.random.fold_in(own, 1), rows)]
    turn = jax.random.randint(jax.random.fold_in(own, 2), (rows, 1), 0, top)
    return jnp.take_along_axis(table, (jnp.arange(top)[None, :] + turn) % top, axis=1)


def shares(number_of, total, most, lean, full):
    weights = [(1 << 20) // math.isqrt(standing ** lean) + 1 for standing in range(1, number_of + 1)]
    largest = most if full else min(most, max(-(-total // number_of), total * weights[0] // sum(weights)))
    least = 1 if total - largest >= number_of - 1 else 0
    holding, surplus = [largest] + [least] * (number_of - 1), total - largest - least * (number_of - 1)
    while surplus > 0:
        candidates = [i for i in range(1, number_of) if holding[i] < largest] or [i for i in range(1, number_of) if holding[i] < most]
        whole, left = sum([weights[i] for i in candidates]), surplus
        for i in candidates:
            addition = min(most - holding[i], max(1, left * weights[i] // whole), surplus)
            holding[i] = holding[i] + addition
            surplus = surplus - addition
    return np.array(holding)


def noise(stream_key, shape, width, limit, pieces=(), kind=jnp.bfloat16):
    entries = jax.random.normal(stream_key, shape, jnp.float32) * width
    if len(pieces) > 0:
        entries = level_of(stream_key, shape, pieces, -0.22, 0.18) * entries
    return jnp.clip(entries, min=-limit, max=limit).astype(kind)


def setup_inputs(seed: int = 0) -> dict:
    arg_keys = jax.random.split(jax.random.key(seed), 8)
    flow_blocks = noise(arg_keys[0], (BLOCKS, CB, NV * NT), 1.0, 6.0, ((0, 8),))
    interp_weights = noise(arg_keys[1], (TILES, TILE, SLOTS * CB), (SLOTS * CB) ** -0.5, 0.25, ((0, 32),))
    donor_owner_keys = jax.random.split(jax.random.fold_in(arg_keys[2], 1), (TILES * SLOTS) // (TILE_DEV * SLOTS))
    donor_owner_turns = jax.random.permutation(jax.random.fold_in(arg_keys[2], 3), (TILES * SLOTS) // (TILE_DEV * SLOTS))
    donor_owner = jax.vmap(lambda own, number: assign_block(jax.random.fold_in(arg_keys[2], 2), own, number, TILE_DEV * SLOTS, N_PANEL, 1, CAP, 2))(donor_owner_keys, donor_owner_turns).reshape((TILES * SLOTS, 1))
    donor_block = plant(jax.random.randint(arg_keys[3], (TILES * SLOTS,), 0, GB_DEV), jax.random.fold_in(arg_keys[3], 1), 0, GB_DEV - 1).astype(jnp.int32)
    panel_normals = noise(arg_keys[4], (3, PANELS), (30.0 * PANELS ** -0.5), 3.0, ((1, 32),), jnp.float32)
    panel_points = jnp.clip(jax.random.uniform(arg_keys[5], (3, PANELS), jnp.float32, -1.0, 1.0) * level_of(arg_keys[5], (3, PANELS), ((1, 32),), -0.4, 0.0), -1.0, 1.0)
    observer_points = draw_observer_points(jax.random.fold_in(arg_keys[7], 71), 0)
    return dict(flow_blocks=flow_blocks, interp_weights=interp_weights, donor_owner=donor_owner, donor_block=donor_block, panel_normals=panel_normals, panel_points=panel_points, observer_points=observer_points)


KAPPA = 0.5

def fourier_table(samples, orders):
    sample_ids = jnp.arange(samples, dtype=jnp.int32)
    harmonic = jnp.arange(1, orders + 1, dtype=jnp.int32)
    wrapped = sample_ids[:, None] * harmonic[None, :] % samples
    angles = wrapped.astype(jnp.float32) * (2.0 * math.pi / samples)
    factor = 2.0 / samples
    return jnp.concatenate([factor * jnp.cos(angles), -factor * jnp.sin(angles)], axis=1)

def spectra_of(values, normals, transform, samples):
    panels = values.shape[0]
    fields = values.reshape(panels, NV, samples)
    density = 1.0 + fields[:, 0]
    velocity = fields[:, 1:4]
    pressure_pert = fields[:, 4]
    normal_vec = jnp.transpose(normals)[:, :, None]
    normal_flow = lax.optimization_barrier(jnp.sum(velocity * normal_vec, axis=1))
    mass_flux = density * normal_flow
    loading = pressure_pert[:, None, :] * normal_vec + mass_flux[:, None, :] * velocity
    series = jnp.concatenate([mass_flux[:, None, :], loading], axis=1)
    return jnp.einsum('pct,tk->ckp', series, transform, precision=lax.Precision.HIGHEST)

def radiate(spectra, points, observers):
    orders = spectra.shape[1] // 2
    offset_vec = observers[:, None, :] - points[:, :, None]
    distance = jnp.sqrt(lax.optimization_barrier(jnp.sum(offset_vec * offset_vec, axis=0)))
    inverse = 1.0 / distance
    direction = offset_vec * inverse[None]
    wavenum = (KAPPA * jnp.arange(1, orders + 1, dtype=jnp.float32))[:, None, None]
    load_re = spectra[1, :orders][:, :, None] * direction[0][None] + spectra[2, :orders][:, :, None] * direction[1][None] + spectra[3, :orders][:, :, None] * direction[2][None]
    load_im = spectra[1, orders:][:, :, None] * direction[0][None] + spectra[2, orders:][:, :, None] * direction[1][None] + spectra[3, orders:][:, :, None] * direction[2][None]
    amp_re = load_re * inverse[None] - wavenum * (spectra[0, orders:][:, :, None] + load_im)
    amp_im = load_im * inverse[None] + wavenum * (spectra[0, :orders][:, :, None] + load_re)
    phase = wavenum * distance[None]
    cosines = jnp.cos(phase)
    sines = jnp.sin(phase)
    spreading = (inverse / (4.0 * math.pi))[None]
    real_part = lax.optimization_barrier(jnp.sum((amp_re * cosines + amp_im * sines) * spreading, axis=1))
    imag_part = lax.optimization_barrier(jnp.sum((amp_im * cosines - amp_re * sines) * spreading, axis=1))
    return jnp.concatenate([real_part, imag_part], axis=0)

def reference(flow_blocks, interp_weights, donor_owner, donor_block, panel_normals, panel_points, observer_points):
    transform = fourier_table(NT, HARM)
    global_block = (donor_owner[:, 0] * GB_DEV + donor_block).astype(jnp.int32).reshape(TILES, SLOTS)
    normals_tiled = panel_normals.reshape(3, TILES, TILE).transpose(1, 0, 2)
    points_tiled = panel_points.reshape(3, TILES, TILE).transpose(1, 0, 2)

    def one_tile(running, tile_data):
        block_ids, weight_tile, normal_tile, point_tile = tile_data
        donors = flow_blocks[block_ids].reshape(SLOTS * CB, NV * NT)
        values = jnp.dot(weight_tile, donors, preferred_element_type=jnp.float32)
        spectra = spectra_of(values, normal_tile, transform, NT)
        return (running + radiate(spectra, point_tile, observer_points), None)
    initial = jnp.zeros((2 * HARM, OBS), jnp.float32)
    running, _ = lax.scan(one_tile, initial, (global_block, interp_weights, normals_tiled, points_tiled))
    return running
```

```python
import math

import jax
import jax.numpy as jnp
from jax import lax
from jax.experimental import pallas as pl
from jax.experimental.pallas import tpu as pltpu
from jax.sharding import PartitionSpec as P

NV = 5
NT = 256
HARM = 64


KAPPA = 0.5


def fourier_table(samples, orders):
    sample_ids = jnp.arange(samples, dtype=jnp.int32)
    harmonic = jnp.arange(1, orders + 1, dtype=jnp.int32)
    wrapped = sample_ids[:, None] * harmonic[None, :] % samples
    angles = wrapped.astype(jnp.float32) * (2.0 * math.pi / samples)
    factor = 2.0 / samples
    return jnp.concatenate([factor * jnp.cos(angles), -factor * jnp.sin(angles)], axis=1)


def spectra_of(values, normals, transform, samples):
    panels = values.shape[0]
    fields = values.reshape(panels, NV, samples)
    density = 1.0 + fields[:, 0]
    velocity = fields[:, 1:4]
    pressure_pert = fields[:, 4]
    normal_vec = jnp.transpose(normals)[:, :, None]
    normal_flow = jnp.sum(velocity * normal_vec, axis=1)
    mass_flux = density * normal_flow
    loading = pressure_pert[:, None, :] * normal_vec + mass_flux[:, None, :] * velocity
    series = jnp.concatenate([mass_flux[:, None, :], loading], axis=1)
    return jnp.einsum("pct,tk->cpk", series, transform, precision=lax.Precision.HIGHEST)


GROUP = 8
SLOT = 8


def sin_cos(angle):
    turns = jnp.floor(angle * (2.0 / math.pi) + 0.5)
    reduced = angle - turns * 1.5703125
    reduced = reduced - turns * 4.837512969970703125e-4
    reduced = reduced - turns * 7.54978995489188216e-8
    square = reduced * reduced
    sine = ((-1.9515295891e-4 * square + 8.3321608736e-3) * square - 1.6666654611e-1) * square * reduced + reduced
    cosine = ((2.443315711809948e-5 * square - 1.388731625493765e-3) * square + 4.166664568298827e-2) * square * square - 0.5 * square + 1.0
    quadrant = turns.astype(jnp.int32)
    swap = (quadrant & 1) == 1
    out_sin = jnp.where(swap, cosine, sine)
    out_cos = jnp.where(swap, sine, cosine)
    out_sin = jnp.where((quadrant & 2) == 2, -out_sin, out_sin)
    out_cos = jnp.where(((quadrant + 1) & 2) == 2, -out_cos, out_cos)
    return out_sin, out_cos


def split_hi_lo(array):
    high = array.astype(jnp.bfloat16).astype(jnp.float32)
    return high, array - high


def geometry(points, observers, cos_ref, sin_ref):
    offsets = [observers[i : i + 1, :] - points[:, i : i + 1] for i in range(3)]
    squared = offsets[0] * offsets[0] + offsets[1] * offsets[1] + offsets[2] * offsets[2]
    distance = jnp.sqrt(squared)
    inverse = 1.0 / distance
    weight = inverse * (1.0 / (4.0 * math.pi))
    far = [offset * (inverse * weight) for offset in offsets]
    near = [term * inverse for term in far]
    slots = near + far + [weight, jnp.zeros_like(weight)]
    high, low = split_hi_lo(jnp.concatenate(slots, axis=0))
    right = jnp.concatenate([high, high, low, low], axis=0).astype(jnp.bfloat16)
    sine, cosine = sin_cos(KAPPA * distance)
    twice = 2.0 * cosine
    past_cos, past_sin = jnp.ones_like(cosine), jnp.zeros_like(sine)
    for order in range(8):
        cos_ref[order] = cosine
        sin_ref[order] = sine
        cosine, past_cos = twice * cosine - past_cos, cosine
        sine, past_sin = twice * sine - past_sin, sine
    return right


def amplitude(left, right, out_ref):
    lanes = lax.broadcasted_iota(jnp.int32, (1, left.shape[1]), 1) % GROUP
    rows = left.shape[0]
    masked = [left * (lanes == y).astype(jnp.float32).astype(jnp.bfloat16) for y in range(GROUP)]
    stacked = jnp.concatenate(masked, axis=0)
    out_ref[...] = jnp.dot(stacked, right, preferred_element_type=jnp.float32)


def accumulate(amp_ref, cos_ref, sin_ref, acc_ref):
    rows, observers = acc_ref.shape
    orders = rows // 2
    blocks = orders // 8
    for half in range(observers // 128):
        lane = pl.ds(half * 128, 128)
        acc_re = [acc_ref[pl.ds(8 * b, 8), lane] for b in range(blocks)]
        acc_im = [acc_ref[pl.ds(orders + 8 * b, 8), lane] for b in range(blocks)]
        for y in range(GROUP):
            cosine = cos_ref[:, y, lane]
            sine = sin_ref[:, y, lane]
            step_cos = cos_ref[7, pl.ds(y, 1), lane]
            step_sin = sin_ref[7, pl.ds(y, 1), lane]
            twice = 2.0 * step_cos
            past_cos = past_sin = None
            for b in range(blocks):
                amp_re = amp_ref[pl.ds(y * rows + 8 * b, 8), lane]
                amp_im = amp_ref[pl.ds(y * rows + orders + 8 * b, 8), lane]
                acc_re[b] = acc_re[b] + (amp_re * cosine + amp_im * sine)
                acc_im[b] = acc_im[b] + (amp_im * cosine - amp_re * sine)
                if b == 0:
                    next_cos = cosine * step_cos - sine * step_sin
                    next_sin = sine * step_cos + cosine * step_sin
                else:
                    next_cos = twice * cosine - past_cos
                    next_sin = twice * sine - past_sin
                past_cos, past_sin, cosine, sine = cosine, sine, next_cos, next_sin
        for b in range(blocks):
            acc_ref[pl.ds(8 * b, 8), lane] = acc_re[b]
            acc_ref[pl.ds(orders + 8 * b, 8), lane] = acc_im[b]


def radiate_kernel(coef_ref, points_ref, observer_ref, acc_ref, amp_a, amp_b, cos_a, cos_b, sin_a, sin_b):
    pairs = coef_ref.shape[0]
    observers = observer_ref[...]
    acc_ref[...] = jnp.zeros_like(acc_ref)

    def prepare(pair):
        both = coef_ref[pair]
        half = both.shape[1] // 2
        first = lax.broadcasted_iota(jnp.int32, both.shape, 1) < half
        high, low = split_hi_lo(both)
        left_a = jnp.where(first, high, pltpu.roll(low, half, 1)).astype(jnp.bfloat16)
        left_b = jnp.where(first, pltpu.roll(high, half, 1), low).astype(jnp.bfloat16)
        return jnp.concatenate([left_a, left_a], axis=1), jnp.concatenate([left_b, left_b], axis=1)

    def points_at(group):
        return points_ref[pl.ds(pl.multiple_of(group * GROUP, GROUP), GROUP), :]

    left, _ = prepare(0)
    amplitude(left, geometry(points_at(0), observers, cos_a, sin_a), amp_a)

    @pl.loop(0, pairs)
    def _(pair):
        _, left_b = prepare(pair)
        amplitude(left_b, geometry(points_at(2 * pair + 1), observers, cos_b, sin_b), amp_b)
        accumulate(amp_a, cos_a, sin_a, acc_ref)
        after = jnp.minimum(pair + 1, pairs - 1)
        left_a, _ = prepare(after)
        amplitude(left_a, geometry(points_at(2 * after), observers, cos_a, sin_a), amp_a)
        accumulate(amp_b, cos_b, sin_b, acc_ref)


def radiate_all(spectra, points, observers):
    orders = spectra.shape[2] // 2
    panels = spectra.shape[1]
    wavenum = KAPPA * jnp.arange(1, orders + 1, dtype=jnp.float32)
    turned = jnp.concatenate(
        [-wavenum * spectra[:, :, orders:], wavenum * spectra[:, :, :orders]], axis=2
    )
    slots = jnp.concatenate(
        [spectra[1:4], turned[1:4], turned[0:1], jnp.zeros_like(turned[0:1])], axis=0
    )
    pairs = panels // (2 * GROUP)
    coefs = slots.reshape(SLOT, pairs, 2, GROUP, 2 * orders).transpose(1, 2, 0, 3, 4)
    coefs = coefs.reshape(pairs, 2 * SLOT * GROUP, 2 * orders).transpose(0, 2, 1)
    count = observers.shape[1]
    wave = pltpu.VMEM((8, GROUP, count), jnp.float32)
    amp = pltpu.VMEM((GROUP * 2 * orders, count), jnp.float32)
    return pl.pallas_call(
        radiate_kernel,
        out_shape=jax.ShapeDtypeStruct((2 * orders, count), jnp.float32),
        in_specs=[pl.BlockSpec(memory_space=pltpu.VMEM)] * 3,
        out_specs=pl.BlockSpec(memory_space=pltpu.VMEM),
        scratch_shapes=[amp, amp, wave, wave, wave, wave],
        name="radiate",
    )(coefs, points.T, observers)


def body(
    flow_blocks,
    interp_weights,
    donor_owner,
    donor_block,
    panel_normals,
    panel_points,
    observer_points,
):
    peer_count = lax.axis_size("panel")
    tile_count, tile_width, stencil = interp_weights.shape
    cell_count = flow_blocks.shape[1]
    slot_count = stencil // cell_count
    row_count = tile_count * slot_count
    capacity = max(2, (3 * row_count + 2 * peer_count - 1) // (2 * peer_count))
    owner_of = donor_owner[:, 0]
    matches = (owner_of[:, None] == jnp.arange(peer_count, dtype=jnp.int32)[None, :]).astype(
        jnp.int32
    )
    slot_rank = jnp.sum(jnp.cumsum(matches, axis=0) * matches, axis=1) - 1
    requests = jnp.zeros((peer_count, capacity), jnp.int32).at[owner_of, slot_rank].set(donor_block)
    found = jnp.take(
        flow_blocks,
        lax.all_to_all(requests, "panel", split_axis=0, concat_axis=0, tiled=True),
        axis=0,
    )
    arrived = lax.all_to_all(found, "panel", split_axis=0, concat_axis=0, tiled=True)
    history = arrived.shape[-1]
    flat_rows = arrived.reshape(peer_count * capacity, cell_count, history)
    picked = jnp.take(flat_rows, owner_of * capacity + slot_rank, axis=0)
    donors = picked.reshape(tile_count, stencil, history)
    values = jnp.einsum("tpc,tcv->tpv", interp_weights, donors, preferred_element_type=jnp.float32)
    values = values.reshape(tile_count * tile_width, history)
    transform = fourier_table(NT, HARM)
    spectra = spectra_of(values, panel_normals, transform, NT)
    group_spectra, group_points = (
        lax.all_gather(spectra, "obs", axis=1, tiled=True),
        lax.all_gather(panel_points, "obs", axis=1, tiled=True),
    )
    partial_sum = radiate_all(group_spectra, group_points, observer_points)
    pressure = lax.psum_scatter(partial_sum, "panel", scatter_dimension=0, tiled=True)
    return pressure


def solution(mesh):
    return jax.shard_map(
        body,
        mesh=mesh,
        in_specs=(
            P("panel", None, None),
            P(("panel", "obs"), None, None),
            P(("panel", "obs"), None),
            P(("panel", "obs")),
            P(None, ("panel", "obs")),
            P(None, ("panel", "obs")),
            P(None, "obs"),
        ),
        out_specs=P("panel", "obs"),
        check_vma=False,
    )
```

```python
import functools
import math

import jax
import jax.numpy as jnp
from jax import lax
from jax.experimental import pallas as pl
from jax.experimental.pallas import tpu as pltpu
from jax.sharding import PartitionSpec as P

NV = 5
NT = 256
HARM = 64


KAPPA = 0.5


def fourier_table(samples, orders):
    sample_ids = jnp.arange(samples, dtype=jnp.int32)
    harmonic = jnp.arange(1, orders + 1, dtype=jnp.int32)
    wrapped = sample_ids[:, None] * harmonic[None, :] % samples
    angles = wrapped.astype(jnp.float32) * (2.0 * math.pi / samples)
    factor = 2.0 / samples
    return jnp.concatenate([factor * jnp.cos(angles), -factor * jnp.sin(angles)], axis=1)


def spectra_of(values, normals, transform, samples):
    panels = values.shape[0]
    fields = values.reshape(panels, NV, samples)
    density = 1.0 + fields[:, 0]
    velocity = fields[:, 1:4]
    pressure_pert = fields[:, 4]
    normal_vec = jnp.transpose(normals)[:, :, None]
    normal_flow = jnp.sum(velocity * normal_vec, axis=1)
    mass_flux = density * normal_flow
    loading = pressure_pert[:, None, :] * normal_vec + mass_flux[:, None, :] * velocity
    series = jnp.concatenate([mass_flux[:, None, :], loading], axis=1)
    return jnp.einsum("pct,tk->cpk", series, transform, precision=lax.Precision.HIGHEST)


GROUP = 8
SLOT = 8


def sin_cos(angle):
    turns = jnp.floor(angle * (2.0 / math.pi) + 0.5)
    reduced = angle - turns * 1.5703125
    reduced = reduced - turns * 4.837512969970703125e-4
    reduced = reduced - turns * 7.54978995489188216e-8
    square = reduced * reduced
    sine = ((-1.9515295891e-4 * square + 8.3321608736e-3) * square - 1.6666654611e-1) * square * reduced + reduced
    cosine = ((2.443315711809948e-5 * square - 1.388731625493765e-3) * square + 4.166664568298827e-2) * square * square - 0.5 * square + 1.0
    quadrant = turns.astype(jnp.int32)
    swap = (quadrant & 1) == 1
    out_sin = jnp.where(swap, cosine, sine)
    out_cos = jnp.where(swap, sine, cosine)
    out_sin = jnp.where((quadrant & 2) == 2, -out_sin, out_sin)
    out_cos = jnp.where(((quadrant + 1) & 2) == 2, -out_cos, out_cos)
    return out_sin, out_cos


def split_hi_lo(array):
    high = array.astype(jnp.bfloat16).astype(jnp.float32)
    return high, array - high


def geometry(points, observers, cos_ref, sin_ref):
    offsets = [observers[i : i + 1, :] - points[:, i : i + 1] for i in range(3)]
    squared = offsets[0] * offsets[0] + offsets[1] * offsets[1] + offsets[2] * offsets[2]
    distance = jnp.sqrt(squared)
    inverse = 1.0 / distance
    weight = inverse * (1.0 / (4.0 * math.pi))
    far = [offset * (inverse * weight) for offset in offsets]
    near = [term * inverse for term in far]
    slots = near + far + [weight, jnp.zeros_like(weight)]
    high, low = split_hi_lo(jnp.concatenate(slots, axis=0))
    right = jnp.concatenate([high, high, low, low], axis=0).astype(jnp.bfloat16)
    sine, cosine = sin_cos(KAPPA * distance)
    twice = 2.0 * cosine
    past_cos, past_sin = jnp.ones_like(cosine), jnp.zeros_like(sine)
    for order in range(8):
        cos_ref[order] = cosine
        sin_ref[order] = sine
        cosine, past_cos = twice * cosine - past_cos, cosine
        sine, past_sin = twice * sine - past_sin, sine
    return right


def amplitude(left, right, out_ref):
    lanes = lax.broadcasted_iota(jnp.int32, (1, left.shape[1]), 1) % GROUP
    rows = left.shape[0]
    masked = [left * (lanes == y).astype(jnp.float32).astype(jnp.bfloat16) for y in range(GROUP)]
    stacked = jnp.concatenate(masked, axis=0)
    out_ref[...] = jnp.dot(stacked, right, preferred_element_type=jnp.float32)


def accumulate(amp_ref, cos_ref, sin_ref, acc_ref):
    rows, observers = acc_ref.shape
    orders = rows // 2
    blocks = orders // 8
    for half in range(observers // 128):
        lane = pl.ds(half * 128, 128)
        acc_re = [acc_ref[pl.ds(8 * b, 8), lane] for b in range(blocks)]
        acc_im = [acc_ref[pl.ds(orders + 8 * b, 8), lane] for b in range(blocks)]
        for y in range(GROUP):
            cosine = cos_ref[:, y, lane]
            sine = sin_ref[:, y, lane]
            step_cos = cos_ref[7, pl.ds(y, 1), lane]
            step_sin = sin_ref[7, pl.ds(y, 1), lane]
            twice = 2.0 * step_cos
            past_cos = past_sin = None
            for b in range(blocks):
                amp_re = amp_ref[pl.ds(y * rows + 8 * b, 8), lane]
                amp_im = amp_ref[pl.ds(y * rows + orders + 8 * b, 8), lane]
                acc_re[b] = acc_re[b] + (amp_re * cosine + amp_im * sine)
                acc_im[b] = acc_im[b] + (amp_im * cosine - amp_re * sine)
                if b == 0:
                    next_cos = cosine * step_cos - sine * step_sin
                    next_sin = sine * step_cos + cosine * step_sin
                else:
                    next_cos = twice * cosine - past_cos
                    next_sin = twice * sine - past_sin
                past_cos, past_sin, cosine, sine = cosine, sine, next_cos, next_sin
        for b in range(blocks):
            acc_ref[pl.ds(8 * b, 8), lane] = acc_re[b]
            acc_ref[pl.ds(orders + 8 * b, 8), lane] = acc_im[b]


def radiate_kernel(coef_ref, points_ref, observer_ref, acc_ref, amp_a, amp_b, cos_a, cos_b, sin_a, sin_b):
    pairs = coef_ref.shape[0]
    observers = observer_ref[...]
    acc_ref[...] = jnp.zeros_like(acc_ref)

    def prepare(pair):
        both = coef_ref[pair]
        half = both.shape[1] // 2
        first = lax.broadcasted_iota(jnp.int32, both.shape, 1) < half
        high, low = split_hi_lo(both)
        left_a = jnp.where(first, high, pltpu.roll(low, half, 1)).astype(jnp.bfloat16)
        left_b = jnp.where(first, pltpu.roll(high, half, 1), low).astype(jnp.bfloat16)
        return jnp.concatenate([left_a, left_a], axis=1), jnp.concatenate([left_b, left_b], axis=1)

    def points_at(group):
        return points_ref[pl.ds(pl.multiple_of(group * GROUP, GROUP), GROUP), :]

    left, _ = prepare(0)
    amplitude(left, geometry(points_at(0), observers, cos_a, sin_a), amp_a)

    @pl.loop(0, pairs)
    def _(pair):
        _, left_b = prepare(pair)
        amplitude(left_b, geometry(points_at(2 * pair + 1), observers, cos_b, sin_b), amp_b)
        accumulate(amp_a, cos_a, sin_a, acc_ref)
        after = jnp.minimum(pair + 1, pairs - 1)
        left_a, _ = prepare(after)
        amplitude(left_a, geometry(points_at(2 * after), observers, cos_a, sin_a), amp_a)
        accumulate(amp_b, cos_b, sin_b, acc_ref)


def radiate_all(spectra, points, observers):
    orders = spectra.shape[2] // 2
    panels = spectra.shape[1]
    wavenum = KAPPA * jnp.arange(1, orders + 1, dtype=jnp.float32)
    turned = jnp.concatenate(
        [-wavenum * spectra[:, :, orders:], wavenum * spectra[:, :, :orders]], axis=2
    )
    slots = jnp.concatenate(
        [spectra[1:4], turned[1:4], turned[0:1], jnp.zeros_like(turned[0:1])], axis=0
    )
    pairs = panels // (2 * GROUP)
    coefs = slots.reshape(SLOT, pairs, 2, GROUP, 2 * orders).transpose(1, 2, 0, 3, 4)
    coefs = coefs.reshape(pairs, 2 * SLOT * GROUP, 2 * orders).transpose(0, 2, 1)
    count = observers.shape[1]
    wave = pltpu.VMEM((8, GROUP, count), jnp.float32)
    amp = pltpu.VMEM((GROUP * 2 * orders, count), jnp.float32)
    return pl.pallas_call(
        radiate_kernel,
        out_shape=jax.ShapeDtypeStruct((2 * orders, count), jnp.float32),
        in_specs=[pl.BlockSpec(memory_space=pltpu.VMEM)] * 3,
        out_specs=pl.BlockSpec(memory_space=pltpu.VMEM),
        scratch_shapes=[amp, amp, wave, wave, wave, wave],
        name="radiate",
    )(coefs, points.T, observers)


def swap_kernel(axis, spread, source_ref, out_ref, send_sem, recv_sem, local_sem):
    peers = out_ref.shape[0]
    me = lax.axis_index(axis)
    barrier = pltpu.get_barrier_semaphore()
    for shift in range(1, peers):
        pl.semaphore_signal(
            barrier,
            inc=1,
            device_id={axis: lax.rem(me + shift, peers)},
            device_id_type=pl.DeviceIdType.MESH,
        )
    own = pltpu.make_async_copy(source_ref.at[me] if spread else source_ref, out_ref.at[me], local_sem)
    own.start()
    pl.semaphore_wait(barrier, peers - 1)
    copies = []
    for shift in range(1, peers):
        target = lax.rem(me + shift, peers)
        copy = pltpu.make_async_remote_copy(
            src_ref=source_ref.at[target] if spread else source_ref,
            dst_ref=out_ref.at[me],
            send_sem=send_sem.at[shift],
            recv_sem=recv_sem.at[shift],
            device_id={axis: target},
            device_id_type=pl.DeviceIdType.MESH,
        )
        copy.start()
        copies.append(copy)
    own.wait()
    for copy in copies:
        copy.wait()


def swap(array, axis, spread, number):
    peers = lax.axis_size(axis)
    shape = array.shape if spread else (peers,) + array.shape
    return pl.pallas_call(
        functools.partial(swap_kernel, axis, spread),
        out_shape=jax.ShapeDtypeStruct(shape, array.dtype),
        in_specs=[pl.BlockSpec(memory_space=pltpu.VMEM)],
        out_specs=pl.BlockSpec(memory_space=pltpu.VMEM),
        scratch_shapes=[
            pltpu.SemaphoreType.DMA((peers,)),
            pltpu.SemaphoreType.DMA((peers,)),
            pltpu.SemaphoreType.DMA,
        ],
        compiler_params=pltpu.CompilerParams(collective_id=number, has_side_effects=True),
        name=f"swap{number}",
    )(array)


def hot(condition):
    return condition.astype(jnp.bfloat16)


def body(
    flow_blocks,
    interp_weights,
    donor_owner,
    donor_block,
    panel_normals,
    panel_points,
    observer_points,
):
    peer_count = lax.axis_size("panel")
    me = lax.axis_index("panel")
    tile_count, tile_width, stencil = interp_weights.shape
    held_count, cell_count, history = flow_blocks.shape
    slot_count = stencil // cell_count
    row_count = tile_count * slot_count
    capacity = max(2, (3 * row_count + 2 * peer_count - 1) // (2 * peer_count))
    owner_of = donor_owner[:, 0]
    wanted = swap(jnp.stack([owner_of, donor_block]), "panel", False, 1)
    rows = jnp.arange(row_count, dtype=jnp.int32)
    upto = hot(rows[:, None] <= rows[None, :])
    asked = wanted[:, 0] == me
    rank = jnp.dot(hot(asked), upto, preferred_element_type=jnp.float32).astype(jnp.int32) - 1
    place = jnp.arange(capacity, dtype=jnp.int32)
    chosen = hot(asked[:, None, :] & (rank[:, None, :] == place[None, :, None]))
    named = hot(wanted[:, 1][:, :, None] == jnp.arange(held_count, dtype=jnp.int32)[None, None, :])
    select = jnp.einsum("qsr,qrb->qsb", chosen, named, preferred_element_type=jnp.float32)
    select = select.astype(jnp.bfloat16).reshape(peer_count * capacity, held_count)
    flat = flow_blocks.reshape(held_count, cell_count * history)
    found = jnp.dot(select, flat, preferred_element_type=jnp.float32).astype(jnp.bfloat16)
    arrived = swap(found.reshape(peer_count, capacity, -1), "panel", True, 2)
    arrived = arrived.reshape(peer_count * capacity, -1)
    matches = owner_of[:, None] == jnp.arange(peer_count, dtype=jnp.int32)[None, :]
    counts = jnp.dot(upto.T, hot(matches), preferred_element_type=jnp.float32)
    own_rank = jnp.sum(jnp.where(matches, counts, 0.0), axis=1).astype(jnp.int32) - 1
    target = jnp.repeat(owner_of * capacity + own_rank, cell_count).reshape(tile_count, stencil)
    lines = jnp.arange(peer_count * capacity, dtype=jnp.int32)
    cell_of = jnp.arange(stencil, dtype=jnp.int32) % cell_count
    values = 0.0
    for cell in range(cell_count):
        moved = hot((target[:, :, None] == lines) & (cell_of == cell)[None, :, None])
        weights = jnp.einsum("tpj,tjk->tpk", interp_weights, moved, preferred_element_type=jnp.float32)
        values = values + jnp.einsum(
            "tpk,kv->tpv",
            weights.astype(jnp.bfloat16),
            arrived[:, cell * history : (cell + 1) * history],
            preferred_element_type=jnp.float32,
        )
    values = values.reshape(tile_count * tile_width, history)
    transform = fourier_table(NT, HARM)
    spectra = spectra_of(values, panel_normals, transform, NT)
    padded = jnp.pad(panel_points.T, ((0, 0), (0, spectra.shape[2] - 3)))
    group = swap(jnp.concatenate([spectra, padded[None]], axis=0), "obs", False, 3)
    group = group.transpose(1, 0, 2, 3).reshape(5, -1, group.shape[3])
    partial_sum = radiate_all(group[:4], group[4, :, :3].T, observer_points)
    terms = swap(partial_sum.reshape(peer_count, -1, partial_sum.shape[1]), "panel", True, 4)
    return jnp.sum(terms, axis=0)


def solution(mesh):
    return jax.shard_map(
        body,
        mesh=mesh,
        in_specs=(
            P("panel", None, None),
            P(("panel", "obs"), None, None),
            P(("panel", "obs"), None),
            P(("panel", "obs")),
            P(None, ("panel", "obs")),
            P(None, ("panel", "obs")),
            P(None, "obs"),
        ),
        out_specs=P("panel", "obs"),
        check_vma=False,
    )
```

```python
import functools
import math

import jax
import jax.numpy as jnp
from jax import lax
from jax.experimental import pallas as pl
from jax.experimental.pallas import tpu as pltpu
from jax.sharding import PartitionSpec as P

NV = 5
NT = 256
HARM = 64


KAPPA = 0.5


def fourier_table(samples, orders):
    sample_ids = jnp.arange(samples, dtype=jnp.int32)
    harmonic = jnp.arange(1, orders + 1, dtype=jnp.int32)
    wrapped = sample_ids[:, None] * harmonic[None, :] % samples
    angles = wrapped.astype(jnp.float32) * (2.0 * math.pi / samples)
    factor = 2.0 / samples
    return jnp.concatenate([factor * jnp.cos(angles), -factor * jnp.sin(angles)], axis=1)


def spectra_of(values, normals, transform, samples):
    panels = values.shape[0]
    fields = values.reshape(panels, NV, samples)
    density = 1.0 + fields[:, 0]
    velocity = fields[:, 1:4]
    pressure_pert = fields[:, 4]
    normal_vec = jnp.transpose(normals)[:, :, None]
    normal_flow = jnp.sum(velocity * normal_vec, axis=1)
    mass_flux = density * normal_flow
    loading = pressure_pert[:, None, :] * normal_vec + mass_flux[:, None, :] * velocity
    series = jnp.concatenate([mass_flux[:, None, :], loading], axis=1)
    return jnp.einsum("pct,tk->cpk", series, transform, precision=lax.Precision.HIGHEST)


GROUP = 8
SLOT = 8


def sin_cos(angle):
    turns = jnp.floor(angle * (2.0 / math.pi) + 0.5)
    reduced = angle - turns * 1.5703125
    reduced = reduced - turns * 4.837512969970703125e-4
    reduced = reduced - turns * 7.54978995489188216e-8
    square = reduced * reduced
    sine = ((-1.9515295891e-4 * square + 8.3321608736e-3) * square - 1.6666654611e-1) * square * reduced + reduced
    cosine = ((2.443315711809948e-5 * square - 1.388731625493765e-3) * square + 4.166664568298827e-2) * square * square - 0.5 * square + 1.0
    quadrant = turns.astype(jnp.int32)
    swap = (quadrant & 1) == 1
    out_sin = jnp.where(swap, cosine, sine)
    out_cos = jnp.where(swap, sine, cosine)
    out_sin = jnp.where((quadrant & 2) == 2, -out_sin, out_sin)
    out_cos = jnp.where(((quadrant + 1) & 2) == 2, -out_cos, out_cos)
    return out_sin, out_cos


def split_hi_lo(array):
    high = array.astype(jnp.bfloat16).astype(jnp.float32)
    return high, array - high


def geometry(points, observers, cos_ref, sin_ref):
    offsets = [observers[i : i + 1, :] - points[:, i : i + 1] for i in range(3)]
    squared = offsets[0] * offsets[0] + offsets[1] * offsets[1] + offsets[2] * offsets[2]
    distance = jnp.sqrt(squared)
    inverse = 1.0 / distance
    weight = inverse * (1.0 / (4.0 * math.pi))
    far = [offset * (inverse * weight) for offset in offsets]
    near = [term * inverse for term in far]
    slots = near + far + [weight, jnp.zeros_like(weight)]
    high, low = split_hi_lo(jnp.concatenate(slots, axis=0))
    right = jnp.concatenate([high, high, low, low], axis=0).astype(jnp.bfloat16)
    sine, cosine = sin_cos(KAPPA * distance)
    twice = 2.0 * cosine
    past_cos, past_sin = jnp.ones_like(cosine), jnp.zeros_like(sine)
    for order in range(8):
        cos_ref[order] = cosine
        sin_ref[order] = sine
        cosine, past_cos = twice * cosine - past_cos, cosine
        sine, past_sin = twice * sine - past_sin, sine
    return right


def amplitude(left, right, out_ref):
    lanes = lax.broadcasted_iota(jnp.int32, (1, left.shape[1]), 1) % GROUP
    rows = left.shape[0]
    masked = [left * (lanes == y).astype(jnp.float32).astype(jnp.bfloat16) for y in range(GROUP)]
    stacked = jnp.concatenate(masked, axis=0)
    out_ref[...] = jnp.dot(stacked, right, preferred_element_type=jnp.float32)


def accumulate(amp_ref, cos_ref, sin_ref, acc_ref):
    rows, observers = acc_ref.shape
    orders = rows // 2
    blocks = orders // 8
    for half in range(observers // 128):
        lane = pl.ds(half * 128, 128)
        acc_re = [acc_ref[pl.ds(8 * b, 8), lane] for b in range(blocks)]
        acc_im = [acc_ref[pl.ds(orders + 8 * b, 8), lane] for b in range(blocks)]
        for y in range(GROUP):
            cosine = cos_ref[:, y, lane]
            sine = sin_ref[:, y, lane]
            step_cos = cos_ref[7, pl.ds(y, 1), lane]
            step_sin = sin_ref[7, pl.ds(y, 1), lane]
            twice = 2.0 * step_cos
            past_cos = past_sin = None
            for b in range(blocks):
                amp_re = amp_ref[pl.ds(y * rows + 8 * b, 8), lane]
                amp_im = amp_ref[pl.ds(y * rows + orders + 8 * b, 8), lane]
                acc_re[b] = acc_re[b] + (amp_re * cosine + amp_im * sine)
                acc_im[b] = acc_im[b] + (amp_im * cosine - amp_re * sine)
                if b == 0:
                    next_cos = cosine * step_cos - sine * step_sin
                    next_sin = sine * step_cos + cosine * step_sin
                else:
                    next_cos = twice * cosine - past_cos
                    next_sin = twice * sine - past_sin
                past_cos, past_sin, cosine, sine = cosine, sine, next_cos, next_sin
        for b in range(blocks):
            acc_ref[pl.ds(8 * b, 8), lane] = acc_re[b]
            acc_ref[pl.ds(orders + 8 * b, 8), lane] = acc_im[b]


def radiate_kernel(coef_ref, points_ref, observer_ref, acc_ref, amp_a, amp_b, cos_a, cos_b, sin_a, sin_b):
    pairs = coef_ref.shape[0]
    observers = observer_ref[...]
    acc_ref[...] = jnp.zeros_like(acc_ref)

    def prepare(pair):
        both = coef_ref[pair]
        half = both.shape[1] // 2
        first = lax.broadcasted_iota(jnp.int32, both.shape, 1) < half
        high, low = split_hi_lo(both)
        left_a = jnp.where(first, high, pltpu.roll(low, half, 1)).astype(jnp.bfloat16)
        left_b = jnp.where(first, pltpu.roll(high, half, 1), low).astype(jnp.bfloat16)
        return jnp.concatenate([left_a, left_a], axis=1), jnp.concatenate([left_b, left_b], axis=1)

    def points_at(group):
        return points_ref[pl.ds(pl.multiple_of(group * GROUP, GROUP), GROUP), :]

    left, _ = prepare(0)
    amplitude(left, geometry(points_at(0), observers, cos_a, sin_a), amp_a)

    @pl.loop(0, pairs)
    def _(pair):
        _, left_b = prepare(pair)
        amplitude(left_b, geometry(points_at(2 * pair + 1), observers, cos_b, sin_b), amp_b)
        accumulate(amp_a, cos_a, sin_a, acc_ref)
        after = jnp.minimum(pair + 1, pairs - 1)
        left_a, _ = prepare(after)
        amplitude(left_a, geometry(points_at(2 * after), observers, cos_a, sin_a), amp_a)
        accumulate(amp_b, cos_b, sin_b, acc_ref)


def radiate_all(spectra, points, observers):
    orders = spectra.shape[2] // 2
    panels = spectra.shape[1]
    wavenum = KAPPA * jnp.arange(1, orders + 1, dtype=jnp.float32)
    turned = jnp.concatenate(
        [-wavenum * spectra[:, :, orders:], wavenum * spectra[:, :, :orders]], axis=2
    )
    slots = jnp.concatenate(
        [spectra[1:4], turned[1:4], turned[0:1], jnp.zeros_like(turned[0:1])], axis=0
    )
    pairs = panels // (2 * GROUP)
    coefs = slots.reshape(SLOT, pairs, 2, GROUP, 2 * orders).transpose(1, 2, 0, 3, 4)
    coefs = coefs.reshape(pairs, 2 * SLOT * GROUP, 2 * orders).transpose(0, 2, 1)
    count = observers.shape[1]
    wave = pltpu.VMEM((8, GROUP, count), jnp.float32)
    amp = pltpu.VMEM((GROUP * 2 * orders, count), jnp.float32)
    return pl.pallas_call(
        radiate_kernel,
        out_shape=jax.ShapeDtypeStruct((2 * orders, count), jnp.float32),
        in_specs=[pl.BlockSpec(memory_space=pltpu.VMEM)] * 3,
        out_specs=pl.BlockSpec(memory_space=pltpu.VMEM),
        scratch_shapes=[amp, amp, wave, wave, wave, wave],
        name="radiate",
    )(coefs, points.T, observers)


def total_kernel(axis, source_ref, sum_ref, held_ref, send_sem, recv_sem, local_sem):
    swap_kernel(axis, True, source_ref, held_ref, send_sem, recv_sem, local_sem)
    total = held_ref[0]
    for peer in range(1, held_ref.shape[0]):
        total = total + held_ref[peer]
    sum_ref[...] = total


def swap_kernel(axis, spread, source_ref, out_ref, send_sem, recv_sem, local_sem):
    peers = out_ref.shape[0]
    me = lax.axis_index(axis)
    barrier = pltpu.get_barrier_semaphore()
    for shift in range(1, peers):
        pl.semaphore_signal(
            barrier,
            inc=1,
            device_id={axis: lax.rem(me + shift, peers)},
            device_id_type=pl.DeviceIdType.MESH,
        )
    own = pltpu.make_async_copy(source_ref.at[me] if spread else source_ref, out_ref.at[me], local_sem)
    own.start()
    pl.semaphore_wait(barrier, peers - 1)
    copies = []
    for shift in range(1, peers):
        target = lax.rem(me + shift, peers)
        copy = pltpu.make_async_remote_copy(
            src_ref=source_ref.at[target] if spread else source_ref,
            dst_ref=out_ref.at[me],
            send_sem=send_sem.at[shift],
            recv_sem=recv_sem.at[shift],
            device_id={axis: target},
            device_id_type=pl.DeviceIdType.MESH,
        )
        copy.start()
        copies.append(copy)
    own.wait()
    for copy in copies:
        copy.wait()


def swap(array, axis, spread, number):
    peers = lax.axis_size(axis)
    shape = array.shape if spread else (peers,) + array.shape
    return pl.pallas_call(
        functools.partial(swap_kernel, axis, spread),
        out_shape=jax.ShapeDtypeStruct(shape, array.dtype),
        in_specs=[pl.BlockSpec(memory_space=pltpu.VMEM)],
        out_specs=pl.BlockSpec(memory_space=pltpu.VMEM),
        scratch_shapes=[
            pltpu.SemaphoreType.DMA((peers,)),
            pltpu.SemaphoreType.DMA((peers,)),
            pltpu.SemaphoreType.DMA,
        ],
        compiler_params=pltpu.CompilerParams(collective_id=number, has_side_effects=True),
        name=f"swap{number}",
    )(array)


def swap_total(array, axis, number):
    peers = lax.axis_size(axis)
    return pl.pallas_call(
        functools.partial(total_kernel, axis),
        out_shape=jax.ShapeDtypeStruct(array.shape[1:], array.dtype),
        in_specs=[pl.BlockSpec(memory_space=pltpu.VMEM)],
        out_specs=pl.BlockSpec(memory_space=pltpu.VMEM),
        scratch_shapes=[
            pltpu.VMEM(array.shape, array.dtype),
            pltpu.SemaphoreType.DMA((peers,)),
            pltpu.SemaphoreType.DMA((peers,)),
            pltpu.SemaphoreType.DMA,
        ],
        compiler_params=pltpu.CompilerParams(collective_id=number, has_side_effects=True),
        name=f"swap{number}",
    )(array)


def hot(condition):
    return condition.astype(jnp.bfloat16)


def body(
    flow_blocks,
    interp_weights,
    donor_owner,
    donor_block,
    panel_normals,
    panel_points,
    observer_points,
):
    peer_count = lax.axis_size("panel")
    me = lax.axis_index("panel")
    tile_count, tile_width, stencil = interp_weights.shape
    held_count, cell_count, history = flow_blocks.shape
    slot_count = stencil // cell_count
    row_count = tile_count * slot_count
    capacity = max(2, (3 * row_count + 2 * peer_count - 1) // (2 * peer_count))
    owner_of = donor_owner[:, 0]
    wanted = swap(jnp.stack([owner_of, donor_block]), "panel", False, 1)
    rows = jnp.arange(row_count, dtype=jnp.int32)
    upto = hot(rows[:, None] <= rows[None, :])
    asked = wanted[:, 0] == me
    rank = jnp.dot(hot(asked), upto, preferred_element_type=jnp.float32).astype(jnp.int32) - 1
    place = jnp.arange(capacity, dtype=jnp.int32)
    chosen = hot(asked[:, None, :] & (rank[:, None, :] == place[None, :, None]))
    named = hot(wanted[:, 1][:, :, None] == jnp.arange(held_count, dtype=jnp.int32)[None, None, :])
    select = jnp.einsum("qsr,qrb->qsb", chosen, named, preferred_element_type=jnp.float32)
    select = select.astype(jnp.bfloat16).reshape(peer_count * capacity, held_count)
    flat = flow_blocks.reshape(held_count, cell_count * history)
    found = jnp.dot(select, flat, preferred_element_type=jnp.float32).astype(jnp.bfloat16)
    arrived = swap(found.reshape(peer_count, capacity, -1), "panel", True, 2)
    arrived = arrived.reshape(peer_count * capacity, -1)
    matches = owner_of[:, None] == jnp.arange(peer_count, dtype=jnp.int32)[None, :]
    counts = jnp.dot(upto.T, hot(matches), preferred_element_type=jnp.float32)
    own_rank = jnp.sum(jnp.where(matches, counts, 0.0), axis=1).astype(jnp.int32) - 1
    target = jnp.repeat(owner_of * capacity + own_rank, cell_count).reshape(tile_count, stencil)
    lines = jnp.arange(peer_count * capacity, dtype=jnp.int32)
    cell_of = jnp.arange(stencil, dtype=jnp.int32) % cell_count
    values = 0.0
    for cell in range(cell_count):
        moved = hot((target[:, :, None] == lines) & (cell_of == cell)[None, :, None])
        weights = jnp.einsum("tpj,tjk->tpk", interp_weights, moved, preferred_element_type=jnp.float32)
        values = values + jnp.einsum(
            "tpk,kv->tpv",
            weights.astype(jnp.bfloat16),
            arrived[:, cell * history : (cell + 1) * history],
            preferred_element_type=jnp.float32,
        )
    values = values.reshape(tile_count * tile_width, history)
    transform = fourier_table(NT, HARM)
    spectra = spectra_of(values, panel_normals, transform, NT)
    series_count, panels, lanes = spectra.shape
    padded = jnp.pad(panel_points, ((0, 5), (0, 0))).reshape(-1, lanes)
    packed = jnp.concatenate([spectra.reshape(-1, lanes), padded], axis=0)
    group = swap(packed, "obs", False, 3)
    cut = series_count * panels
    all_spectra = group[:, :cut].reshape(-1, series_count, panels, lanes).transpose(1, 0, 2, 3)
    all_spectra = all_spectra.reshape(series_count, -1, lanes)
    all_points = group[:, cut:].reshape(-1, 8, panels)[:, :3].transpose(1, 0, 2).reshape(3, -1)
    partial_sum = radiate_all(all_spectra, all_points, observer_points)
    terms = partial_sum.reshape(peer_count, -1, partial_sum.shape[1])
    return swap_total(terms, "panel", 4)


def solution(mesh):
    return jax.shard_map(
        body,
        mesh=mesh,
        in_specs=(
            P("panel", None, None),
            P(("panel", "obs"), None, None),
            P(("panel", "obs"), None),
            P(("panel", "obs")),
            P(None, ("panel", "obs")),
            P(None, ("panel", "obs")),
            P(None, "obs"),
        ),
        out_specs=P("panel", "obs"),
        check_vma=False,
    )
```
